32 devices in a mesh: edge: 8 (over z, y), mp: 4 (over x, core).
Axes of the slice: x: 2, y: 2, z: 4, core: 2. Of those that a mesh axis runs over, the one named last changes fastest.
Arguments:
- edge_feat: bfloat16 [16384, 512], P('edge', 'mp'), may hold values from -6 to 6
- mirror_rows: int32 [16384], P('edge'), may hold values from 0 to 2047, as said below
- edge_slot: int32 [128, 128], P('edge'), may hold values from 0 to 15
- group_owner: int32 [512, 1], P('edge'), may hold values from 0 to 7; in each aligned block of 64 rows (0 to 63, 64 to 127, ...) at most 16 rows name the same one
- group_window: int32 [512], P('edge'), may hold values from 0 to 127
- up_edge: bfloat16 [512, 512], P(None, 'mp'), may hold values from -0.25 to 0.25
- down_edge: bfloat16 [512, 512], P('mp'), may hold values from -0.25 to 0.25
- mix_self: bfloat16 [512, 512], P(None, 'mp'), may hold values from -0.1875 to 0.1875
- mix_mirror: bfloat16 [512, 512], P(None, 'mp'), may hold values from -0.1875 to 0.1875
- up_atom: bfloat16 [512, 512], P(None, 'mp'), may hold values from -0.25 to 0.25
- down_atom: bfloat16 [512, 512], P('mp'), may hold values from -0.25 to 0.25
- atom_gain: float32 [512], replicated, may hold values from 0.1 to 1.9
Outputs:
- atom_out: bfloat16 [16384, 512], P('edge', 'mp')
The draws below stay inside these ranges and needn't reach their ends.
Inputs may be any that keep to these rules, and one draw needn't show every extreme that they name: Within each block of 2048 rows mirror_rows is a permutation; the partner block holds its inverse permutation, so the matching of reverse edges is symmetric. `group_owner`: among the 64 groups of one device, no owner is named more than 16 times, and in every draw some device names some owner exactly 16 times.
All inputs are finite; a program needn't handle non-finite values.
Results may differ from the reference program's by a relative error of at most 0.014.
Values may be sent and summed in bfloat16 or wider, within the bound.
A program may use at most 64 MiB of HBM per device.

```python
import math
import jax
import jax.numpy as jnp
import numpy as np
from jax import lax

D = 512
H = 512
E_DEV = 2048
A_DEV = 2048
GR = 32
AW = 16
HB = 128
CAP = 16
EDGES = 16384
GROUPS = 512
ATOMS = 16384
NW = 128
N_EDGE = 8


def draw_mirror_rows(key, part):
    blocks = EDGES // E_DEV
    half = blocks // 2
    keys = jax.random.split(jax.random.fold_in(key, 17), half)
    forward = jax.vmap(lambda k: jax.random.permutation(k, E_DEV))(keys).astype(jnp.int32)
    inverse = jnp.argsort(forward, axis=1, stable=True).astype(jnp.int32)
    return jnp.concatenate([forward, inverse], axis=0).reshape(EDGES).astype(jnp.int32)


def place_ends(array, key, least, largest):
    spot = [jax.random.randint(jax.random.fold_in(key, axis), (), 0, length) for axis, length in enumerate(array.shape)]
    longest = array.shape.index(max(array.shape))
    neighbour = spot[:longest] + [(spot[longest] + 1) % array.shape[longest]] + spot[longest + 1:]
    return array.at[tuple(spot)].set(least).at[tuple(neighbour)].set(largest)


def levels(stream_key, shape, shards, smallest, top_value):
    gain, own = 1.0, jax.random.fold_in(stream_key, 6)
    for axis_at, blocks in shards:
        heights = jnp.exp(jax.random.uniform(jax.random.fold_in(own, axis_at), (blocks,), jnp.float32, smallest / len(shards), top_value / len(shards)))
        gain = gain * jnp.repeat(heights, shape[axis_at] // blocks).reshape([-1 if axis == axis_at else 1 for axis in range(len(shape))])
    return gain


def routed_block(key, own, number, rows, amount, top, reach, slope):
    order = jax.random.permutation(key, amount)
    packed, common = portions_of(amount, rows * top, reach, slope, True), portions_of(amount, rows * top, reach, slope, False)
    places = jnp.arange(amount)

    def named(tallies, turn):
        used = int((tallies > 0).sum())
        fixed = max(1, used // 4)
        moved = fixed + (places - fixed + turn * (used - fixed)) % max(1, amount - fixed)
        return jnp.zeros((amount,), jnp.int32).at[order[jnp.where(places < fixed, places, moved)]].set(jnp.asarray(tallies, jnp.int32))

    tallies = jnp.where(number % 4 == 0, named(packed, number // 4), named(common, number - number // 4 - 1))
    mixed = jax.random.permutation(jax.random.fold_in(own, 3), amount)
    giver, taker = mixed[0:amount // 2 * 2:2], mixed[1:amount // 2 * 2:2]
    room = jnp.minimum(tallies[giver] - 1, reach - tallies[taker]) // 2
    room = jnp.where((giver == order[0]) | (taker == order[0]) | (tallies[taker] == 0), 0, jnp.maximum(room, 0))
    moved = jax.random.randint(jax.random.fold_in(own, 4), (amount // 2,), 0, 1 << 20) % (room + 1)
    tallies = tallies.at[giver].add(-moved).at[taker].add(moved)
    members = jnp.searchsorted(jnp.cumsum(tallies), jnp.arange(rows * top), side="right").astype(jnp.int32)
    grid = members.reshape(top, rows).T
    grid = grid[jax.random.permutation(jax.random.fold_in(own, 1), rows)]
    turn = jax.random.randint(jax.random.fold_in(own, 2), (rows, 1), 0, top)
    return jnp.take_along_axis(grid, (jnp.arange(top)[None, :] + turn) % top, axis=1)


def portions_of(count, total, most, skew, full):
    portions = [(1 << 20) // math.isqrt(standing ** skew) + 1 for standing in range(1, count + 1)]
    largest = most if full else min(most, max(-(-total // count), total * portions[0] // sum(portions)))
    least = 1 if total - largest >= count - 1 else 0
    given, surplus = [largest] + [least] * (count - 1), total - largest - least * (count - 1)
    while surplus > 0:
        candidates = [i for i in range(1, count) if given[i] < largest] or [i for i in range(1, count) if given[i] < most]
        pool, budget = sum([portions[i] for i in candidates]), surplus
        for i in candidates:
            more = min(most - given[i], max(1, budget * portions[i] // pool), surplus)
            given[i] = given[i] + more
            surplus = surplus - more
    return np.array(given)


def bell_draw(own_key, shape, deviation, limit, cuts=(), kind=jnp.bfloat16):
    result = jax.random.normal(own_key, shape, jnp.float32) * deviation
    if len(cuts) > 0:
        result = levels(own_key, shape, cuts, -0.22, 0.18) * result
    return jnp.clip(result, min=-limit, max=limit).astype(kind)


def setup_inputs(seed: int = 0) -> dict:
    streams_of = jax.random.split(jax.random.key(seed), 13)
    edge_feat = bell_draw(streams_of[0], (EDGES, D), 1.0, 6.0, ((0, 8), (1, 4)))
    mirror_rows = draw_mirror_rows(jax.random.fold_in(streams_of[12], 71), 0)
    edge_slot = place_ends(jax.random.randint(streams_of[2], (EDGES // 128, 128), 0, AW), jax.random.fold_in(streams_of[2], 1), 0, AW - 1).astype(jnp.int32)
    group_owner_keys = jax.random.split(jax.random.fold_in(streams_of[3], 1), GROUPS // (E_DEV // GR))
    group_owner_turns = jax.random.permutation(jax.random.fold_in(streams_of[3], 3), GROUPS // (E_DEV // GR))
    group_owner = jax.vmap(lambda own, number: routed_block(jax.random.fold_in(streams_of[3], 2), own, number, E_DEV // GR, N_EDGE, 1, CAP, 2))(group_owner_keys, group_owner_turns).reshape((GROUPS, 1))
    group_window = place_ends(jax.random.randint(streams_of[4], (GROUPS,), 0, NW), jax.random.fold_in(streams_of[4], 1), 0, NW - 1).astype(jnp.int32)
    up_edge = bell_draw(streams_of[5], (D, H), D ** -0.5, 0.25, ((1, 4),))
    down_edge = bell_draw(streams_of[6], (H, D), H ** -0.5, 0.25, ((0, 4),))
    mix_self = bell_draw(streams_of[7], (D, D), (2 * D) ** -0.5, 0.1875, ((1, 4),))
    mix_mirror = bell_draw(streams_of[8], (D, D), (2 * D) ** -0.5, 0.1875, ((1, 4),))
    up_atom = bell_draw(streams_of[9], (D, H), D ** -0.5, 0.25, ((1, 4),))
    down_atom = bell_draw(streams_of[10], (H, D), H ** -0.5, 0.25, ((0, 4),))
    atom_gain = jnp.clip(1.0 + 0.18 * jax.random.normal(streams_of[11], (D,), jnp.float32), 0.1, 1.9)
    return dict(edge_feat=edge_feat, mirror_rows=mirror_rows, edge_slot=edge_slot, group_owner=group_owner, group_window=group_window, up_edge=up_edge, down_edge=down_edge, mix_self=mix_self, mix_mirror=mix_mirror, up_atom=up_atom, down_atom=down_atom, atom_gain=atom_gain)


def blocked_down(hidden, down):
    total = jnp.zeros((hidden.shape[0], down.shape[1]), jnp.float32)
    for k in range(H // HB):
        part = jnp.dot(hidden[:, k * HB:(k + 1) * HB], down[k * HB:(k + 1) * HB], preferred_element_type=jnp.float32)
        total = total + part.astype(jnp.bfloat16).astype(jnp.float32)
    return total

def reference(edge_feat, mirror_rows, edge_slot, group_owner, group_window, up_edge, down_edge, mix_self, mix_mirror, up_atom, down_atom, atom_gain):
    edge_pre = jnp.dot(edge_feat, up_edge, preferred_element_type=jnp.float32)
    edge_hidden = jax.nn.silu(edge_pre).astype(jnp.bfloat16)
    edge_one = (edge_feat.astype(jnp.float32) + blocked_down(edge_hidden, down_edge)).astype(jnp.bfloat16)
    blocks = EDGES // E_DEV
    stacked = edge_one.reshape(blocks, E_DEV, D)
    partner = jnp.bitwise_xor(jnp.arange(blocks, dtype=jnp.int32), blocks // 2)
    mirrored = stacked[partner]
    picks = mirror_rows.reshape(blocks, E_DEV)[:, :, None].astype(jnp.int32)
    reverse = jnp.take_along_axis(mirrored, picks, axis=1).reshape(EDGES, D)
    mixed = jnp.dot(edge_one, mix_self, preferred_element_type=jnp.float32) + jnp.dot(reverse, mix_mirror, preferred_element_type=jnp.float32)
    edge_two = (edge_one.astype(jnp.float32) + jax.nn.silu(mixed)).astype(jnp.bfloat16)
    owner = jnp.repeat(group_owner[:, 0], GR)
    window = jnp.repeat(group_window, GR)
    target = (owner * A_DEV + window * AW + edge_slot.reshape(EDGES)).astype(jnp.int32)
    atom_sum = jax.ops.segment_sum(edge_two.astype(jnp.float32), target, num_segments=ATOMS).astype(jnp.bfloat16)
    atom_f = atom_sum.astype(jnp.float32)
    scale = lax.rsqrt(lax.optimization_barrier(jnp.mean(atom_f * atom_f, axis=1, keepdims=True)) + 1e-06)
    normed = (atom_f * scale * atom_gain.astype(jnp.float32)).astype(jnp.bfloat16)
    atom_hidden = jax.nn.silu(jnp.dot(normed, up_atom, preferred_element_type=jnp.float32)).astype(jnp.bfloat16)
    return (atom_f + blocked_down(atom_hidden, down_atom)).astype(jnp.bfloat16)
```

```python
import functools
import jax
import jax.numpy as jnp
from jax import lax
from jax.experimental import pallas as pl
from jax.experimental.pallas import tpu as pltpu
from jax.sharding import PartitionSpec as P

AW = 16
MESH = pl.DeviceIdType.MESH
F32 = jnp.float32
BF16 = jnp.bfloat16


def iota(shape, dim):
    return lax.broadcasted_iota(jnp.int32, shape, dim)


def one_hot(mask):
    return jnp.where(mask, 1.0, 0.0).astype(BF16)


def dot(a, b):
    return jnp.dot(a, b, preferred_element_type=F32)


def silu(v):
    return v / (1.0 + jnp.exp(-v))


def at(start, size):
    return pl.ds(pl.multiple_of(start, size), size)


def kernel(
    E, M, cap,
    x_in, mirror_in, slot_in, owner_in, window_in,
    up_e, down_e, mix_s, mix_m, up_a, down_a, gain_in,
    out,
    x, mirror, slot, owner_r, window_r, gain,
    perm, own, rev, g_up_e, g_down_e, g_mix_s, g_mix_m, g_up_a, g_down_a,
    one, mixed_self, part, part_cols, idx_send, idx_got, select, block_send, block_got,
    total, atom_rows, updated,
    own_s, own_r, rev_s, rev_r, w_s, w_r, idx_s, idx_r, part_s, part_r,
    block_s, block_r, relay_s, relay_r, out_s, out_r, local_w, local, load,
):
    R, W = x.shape
    Q, D = R // M, W * M
    CH = slot.shape[1]
    NC = Q // CH
    G = owner_r.shape[1]
    GR = R // G
    PR = CH // GR * AW
    NP = NC * PR
    PF = M * NP
    SR = cap * AW
    half = Q // 2
    RH = R // 2
    AC = RH // half
    e, m = lax.axis_index("edge"), lax.axis_index("mp")
    p = e ^ (E // 2)
    side, pair = m % 2, m // 2
    peers = sorted(range(1, M), reverse=True)

    def remote(src, dst, ss, rs, f, j):
        return pltpu.make_async_remote_copy(
            src_ref=src, dst_ref=dst, send_sem=ss, recv_sem=rs,
            device_id=(f, j), device_id_type=MESH,
        )

    loads = [
        pltpu.make_async_copy(src, dst, load.at[i])
        for i, (src, dst) in enumerate(
            [
                (mirror_in, mirror), (x_in, x), (owner_in, owner_r),
                (window_in, window_r), (slot_in, slot), (gain_in, gain),
            ]
        )
    ]
    for copy in loads:
        copy.start()

    barrier = pltpu.get_barrier_semaphore()
    for d in peers:
        pl.semaphore_signal(barrier, inc=1, device_id=(p, m ^ d), device_id_type=MESH)
        pl.semaphore_signal(barrier, inc=1, device_id=(e, m ^ d), device_id_type=MESH)

    def greet(d, _):
        pl.semaphore_signal(barrier, inc=1, device_id=(e ^ d, m), device_id_type=MESH)
        return 0

    lax.fori_loop(1, E, greet, 0)

    shards = (up_e, down_e, mix_s, mix_m, up_a, down_a)
    wholes = (g_up_e, g_down_e, g_mix_s, g_mix_m, g_up_a, g_down_a)
    by_rows = (False, True, False, False, False, True)
    bits = [1 << b for b in reversed(range(M.bit_length() - 1))]

    def low_bits(d):
        return [b for b in bits if d == 0 or b < (d & -d)]

    high = [b for b in bits if b > 1]
    even = sorted(range(2, M, 2), key=lambda v: -(v & -v))
    mine, other = e % 2, 1 - e % 2

    def shard_at(k, i):
        if by_rows[k]:
            return wholes[k].at[at(i * W, W), :]
        return wholes[k].at[:, at(i * W, W)]

    def half_at(k, i, h):
        if by_rows[k]:
            return wholes[k].at[pl.ds(pl.multiple_of(i * W + h * (W // 2), W // 2), W // 2), :]
        return wholes[k].at[at(h * (D // 2), D // 2), at(i * W, W)]

    def w_near(k):
        return remote(shards[k], shard_at(k, m), w_s.at[k, 0, 1], w_r.at[k, 1, 0], e, m ^ 1)

    def w_far(k, d, b):
        if d:
            src = half_at(k, m ^ d, mine)
        else:
            rows = shards[k].shape[0] // 2
            src = shards[k].at[at(mine * rows, rows), :]
        return remote(
            src, half_at(k, m ^ d, mine), w_s.at[k, d, b], w_r.at[k, d ^ b, 0], e, m ^ b
        )

    def w_swap(k, d):
        ref = half_at(k, m ^ d, mine)
        return remote(ref, ref, w_s.at[k, d, M], w_r.at[k, d, 1], e ^ 1, m)

    def w_pass(k, d, j):
        ref = half_at(k, m ^ d, other if j else mine)
        return remote(ref, ref, w_s.at[k, d, M + 1 + j], w_r.at[k, d ^ 1, j], e, m ^ 1)

    def w_own(k):
        return pltpu.make_async_copy(shards[k], shard_at(k, m), local_w.at[k])

    def w_start(k):
        for b in high:
            w_far(k, 0, b).start()
        w_near(k).start()

    def w_finish(k):
        for d in even:
            b = d & -d
            w_far(k, d ^ b, b).wait_recv()
            w_swap(k, d).start()
            for c in high:
                if c < b:
                    w_far(k, d, c).start()
            w_pass(k, d, 0).start()

    def w_second(k):
        for d in even:
            w_swap(k, d).wait_recv()
            w_pass(k, d, 1).start()

    def w_wait(k):
        w_own(k).wait()
        w_near(k).wait_recv()
        for d in even:
            for j in range(2):
                w_pass(k, d, j).wait_recv()

    def w_drain(k):
        w_near(k).wait_send()
        for b in high:
            w_far(k, 0, b).wait_send()
        for d in even:
            w_swap(k, d).wait_send()
            for c in high:
                if c < (d & -d):
                    w_far(k, d, c).wait_send()
            for j in range(2):
                w_pass(k, d, j).wait_send()

    for k in range(6):
        w_own(k).start()

    def own_local():
        return pltpu.make_async_copy(x_in.at[at(m * Q, Q), :], own.at[:, at(m * W, W)], local.at[0])

    def own_copy(d):
        return remote(
            x_in.at[at((m ^ d) * Q, Q), :], own.at[:, at(m * W, W)],
            own_s.at[d], own_r.at[d], e, m ^ d,
        )

    own_local().start()

    def rev_build(c):
        for j in range(M):
            rows = j * Q + c * CH
            picks = one_hot(iota((CH, R), 0) + rows == mirror[...])
            perm[at(rows, CH), :] = dot(picks, x[...]).astype(BF16)

    def rev_copy(c, d):
        j = m ^ d
        return remote(
            perm.at[at(j * Q + c * CH, CH), :], rev.at[at(c * CH, CH), at(m * W, W)],
            rev_s.at[d, c], rev_r.at[d, c], p, j,
        )

    def rev_start(c):
        for d in [0] + peers[::-1]:
            rev_copy(c, d).start()

    for copy in loads:
        copy.wait()

    diag = iota((G, G), 0) == iota((G, G), 1)
    owner_c = jnp.sum(jnp.where(diag, owner_r[...], 0), axis=1, keepdims=True)
    k_g = lax.div(iota((G, G * AW), 1), AW)
    row_g = iota((G, G * AW), 0)
    owner_k = jnp.sum(jnp.where(k_g == row_g, owner_c, 0), axis=0, keepdims=True)
    rank_k = jnp.sum(
        jnp.where((owner_c == owner_k) & (row_g < k_g), 1, 0), axis=0, keepdims=True
    )
    target = (owner_k * cap + rank_k) * AW + lax.rem(iota((1, G * AW), 1), AW)
    window_c = jnp.sum(jnp.where(diag, window_r[...], 0), axis=1, keepdims=True)
    rank_c = jnp.sum(
        jnp.where((owner_c == owner_r[...]) & (iota((G, G), 1) < iota((G, G), 0)), 1, 0),
        axis=1, keepdims=True,
    )
    place_c = owner_c * cap + rank_c

    def atom_index(f):
        lane = iota((G, SR), 1)
        hit = place_c == f * cap + lax.div(lane, AW)
        value = jnp.sum(
            jnp.where(hit, window_c * AW + lax.rem(lane, AW) + 1, 0), axis=0, keepdims=True
        )
        return jnp.broadcast_to(value - 1, (8, SR))

    def idx_build(d, _):
        idx_send[e ^ d] = atom_index(e ^ d)
        return 0

    lax.fori_loop(1, E, idx_build, 0)
    idx_got[e] = atom_index(e)
    rev_build(0)

    pl.semaphore_wait(barrier, E - 1 + 2 * (M - 1))

    rev_start(0)
    for d in peers:
        own_copy(d).start()
    for c in range(1, NC):
        rev_build(c)
        rev_start(c)
        for k in (2 * c - 2, 2 * c - 1):
            if k < 6:
                w_start(k)
    for k in range(max(0, 2 * NC - 2), 6):
        w_start(k)

    def idx_copy(d):
        return remote(
            idx_send.at[e ^ d], idx_got.at[e], idx_s.at[d], idx_r.at[d], e ^ d, m
        )

    def idx_start(d, _):
        idx_copy(d).start()
        return 0

    lax.fori_loop(1, E, idx_start, 0)

    def select_build(f, _):
        select[at(f * SR, SR), :] = one_hot(iota((SR, PF), 0) + f * SR == target)
        return 0

    lax.fori_loop(0, E, select_build, 0)
    w_finish(0)
    w_finish(1)
    own_local().wait()
    for d in peers:
        own_copy(d).wait_recv()
    w_second(0)
    w_second(1)
    w_wait(0)
    w_wait(1)

    def edge_rows(rows):
        hidden = silu(dot(rows, g_up_e[...])).astype(BF16)
        return (rows.astype(F32) + dot(hidden, g_down_e[...])).astype(BF16)

    def own_step(i, _):
        one[at(i * half, half), :] = edge_rows(own[at(i * half, half), :])
        return 0

    lax.fori_loop(0, 2, own_step, 0)
    w_finish(2)
    w_finish(3)
    w_second(2)
    w_second(3)
    w_wait(2)

    def self_step(i, _):
        mixed_self[at(i * half, half), :] = dot(one[at(i * half, half), :], g_mix_s[...])
        return 0

    lax.fori_loop(0, 2, self_step, 0)
    w_wait(3)

    def part_copy(c, d):
        return remote(
            part.at[at(c * PR, PR), at((m ^ d) * W, W)],
            part_cols.at[at(m * NP + c * PR, PR), :],
            part_s.at[d, c], part_r.at[d, c], e, m ^ d,
        )

    def part_local(c):
        return pltpu.make_async_copy(
            part.at[at(c * PR, PR), at(m * W, W)],
            part_cols.at[at(m * NP + c * PR, PR), :], part_s.at[0, c],
        )

    def edge_step(c, _):
        for d in peers + [0]:
            rev_copy(c, d).wait_recv()
        rows = at(c * CH, CH)
        reverse = edge_rows(rev[rows, :])
        mixed = mixed_self[rows, :] + dot(reverse, g_mix_m[...])
        two = (one[rows, :].astype(F32) + silu(mixed)).astype(BF16)
        spot = lax.div(iota((PR, CH), 1), GR) * AW + slot[pl.ds(m * NC + c, 1), :]
        part[at(c * PR, PR), :] = dot(one_hot(iota((PR, CH), 0) == spot), two).astype(BF16)
        part_local(c).start()
        for d in peers:
            part_copy(c, d).start()
        return 0

    lax.fori_loop(0, NC - 1, edge_step, 0)
    w_finish(4)
    w_finish(5)
    w_second(4)
    w_second(5)
    edge_step(NC - 1, 0)

    def part_wait(c, _):
        part_local(c).wait()
        for d in peers:
            part_copy(c, d).wait_recv()
        return 0

    lax.fori_loop(0, NC, part_wait, 0)

    def owner_block(f):
        return dot(select[at(f * SR, SR), :], part_cols[...]).astype(BF16)

    def block_at(f, i):
        return block_got.at[at(f * SR, SR), at(i * W, W)]

    def block_copy(d):
        return remote(
            block_send.at[e ^ d], block_at(e, m), block_s.at[d], block_r.at[d], e ^ d, m
        )

    def block_step(d, _):
        block_send[e ^ d] = owner_block(e ^ d)
        block_copy(d).start()
        return 0

    lax.fori_loop(1, E, block_step, 0)
    block_got[at(e * SR, SR), at(m * W, W)] = owner_block(e)

    hops = [(j, b) for j in range(M) for b in low_bits(j)]

    def relay(d, j, b):
        ref = block_at(e ^ d, m ^ j)
        return remote(
            ref, ref, relay_s.at[d, hops.index((j, b))], relay_r.at[d, j ^ b], e, m ^ b
        )

    def relay_first(d):
        for b in low_bits(0):
            relay(d, 0, b).start()

    def relay_next(d):
        for j in sorted(range(1, M), key=lambda v: -(v & -v)):
            if low_bits(j):
                b = j & -j
                relay(d, j ^ b, b).wait_recv()
                for c in low_bits(j):
                    relay(d, j, c).start()

    def relay_wait(d):
        for j in range(1, M):
            if not low_bits(j):
                b = j & -j
                relay(d, j ^ b, b).wait_recv()

    def arrive(d):
        idx_copy(d).wait_recv()
        block_copy(d).wait_recv()
        relay_first(d)

    def placed(d, start):
        f = e ^ d
        picks = one_hot(iota((half, SR), 0) + start == idx_got[f][:1, :])
        return dot(picks, block_got[at(f * SR, SR), :])

    def gather(i):
        relay_wait(2 * i)
        relay_wait(2 * i + 1)

    def add(i):
        gather(i)

        def add_rows(r, _):
            start = side * RH + r * half
            rows = at(r * half, half)
            total[rows, :] += placed(2 * i, start) + placed(2 * i + 1, start)
            return 0

        lax.fori_loop(0, AC, add_rows, 0)

    def clear(r, _):
        total[at(r * half, half), :] = jnp.zeros((half, D), F32)
        return 0

    relay_first(0)
    lax.fori_loop(0, AC, clear, 0)
    arrive(1)
    last = E // 2 - 1

    def stage(i):
        arrive(2 * i + 2)
        arrive(2 * i + 3)
        relay_next(2 * i)
        relay_next(2 * i + 1)

    def flow(i, _):
        stage(i)
        add(i - 1)
        return 0

    stage(0)
    lax.fori_loop(1, last, flow, 0)
    add(last - 1)
    relay_next(2 * last)
    relay_next(2 * last + 1)
    w_wait(4)
    w_wait(5)
    gather(last)

    def out_rows(r, s):
        return out.at[at(s * RH + r * half, half), :]

    def out_copy(r):
        return remote(
            updated.at[at(r * half, half), at((1 - side) * W, W)], out_rows(r, side),
            out_s.at[1, r], out_r.at[r], e, m ^ 1,
        )

    def out_local(r):
        return pltpu.make_async_copy(
            updated.at[at(r * half, half), at(side * W, W)], out_rows(r, side), out_s.at[0, r]
        )

    def atom_step(r, _):
        rows = at(r * half, half)
        start = side * RH + r * half
        sums = total[rows, :] + (placed(2 * last, start) + placed(2 * last + 1, start))
        atom_rows[rows, :] = sums.astype(BF16)
        atoms = atom_rows[rows, :].astype(F32)
        scale = lax.rsqrt(jnp.sum(atoms * atoms, axis=1, keepdims=True) / D + 1e-06)
        normed = (atoms * scale * gain[...]).astype(BF16)
        hidden = silu(dot(normed, g_up_a[...])).astype(BF16)
        columns = at(pair * (2 * W), 2 * W)
        kept = atom_rows[rows, columns].astype(F32)
        updated[rows, :] = (kept + dot(hidden, g_down_a[:, columns])).astype(BF16)
        out_copy(r).start()
        out_local(r).start()
        return 0

    lax.fori_loop(0, AC, atom_step, 0)

    for d in peers:
        own_copy(d).wait_send()
    for k in range(6):
        w_drain(k)

    def drain_chunk(c, _):
        for d in peers + [0]:
            rev_copy(c, d).wait_send()
        for d in peers:
            part_copy(c, d).wait_send()
        return 0

    lax.fori_loop(0, NC, drain_chunk, 0)

    def drain_relay(d):
        for j, b in hops:
            relay(d, j, b).wait_send()

    def drain_owner(d, _):
        idx_copy(d).wait_send()
        block_copy(d).wait_send()
        drain_relay(d)
        return 0

    drain_relay(0)
    lax.fori_loop(1, E, drain_owner, 0)
    for r in range(AC):
        out_local(r).wait()
        out_copy(r).wait_send()
        out_copy(r).wait_recv()


def body(E, M, x, mirror, slot, owner, window, up_e, down_e, mix_s, mix_m, up_a, down_a, gain):
    R, W = x.shape
    Q, D = R // M, W * M
    NC = Q // slot.shape[1]
    G = owner.shape[0]
    anywhere = pl.BlockSpec(memory_space=pl.ANY)
    cap = max(2, 2 * G // E)
    SR = cap * AW
    NP = Q // (R // G) * AW
    AC = R // 2 // (Q // 2)
    vmem = pl.BlockSpec(memory_space=pl.ANY)
    dma = pltpu.SemaphoreType.DMA
    return pl.pallas_call(
        functools.partial(kernel, E, M, cap),
        name="edge_window",
        out_shape=jax.ShapeDtypeStruct((R, W), BF16),
        in_specs=[anywhere] * 12,
        out_specs=vmem,
        scratch_shapes=[
            pltpu.VMEM((R, W), BF16),
            pltpu.VMEM((1, R), jnp.int32),
            pltpu.VMEM(slot.shape, jnp.int32),
            pltpu.VMEM((1, G), jnp.int32),
            pltpu.VMEM((1, G), jnp.int32),
            pltpu.VMEM((1, D), F32),
            pltpu.VMEM((R, W), BF16),
            pltpu.VMEM((Q, D), BF16),
            pltpu.VMEM((Q, D), BF16),
        ]
        + [pltpu.VMEM((D, D), BF16)] * 6
        + [
            pltpu.VMEM((Q, D), BF16),
            pltpu.VMEM((Q, D), F32),
            pltpu.VMEM((NP, D), BF16),
            pltpu.VMEM((M * NP, W), BF16),
            pltpu.VMEM((E, 8, SR), jnp.int32),
            pltpu.VMEM((E, 8, SR), jnp.int32),
            pltpu.VMEM((E * SR, M * NP), BF16),
            pltpu.VMEM((E, SR, W), BF16),
            pltpu.VMEM((E * SR, D), BF16),
            pltpu.VMEM((R // 2, D), F32),
            pltpu.VMEM((R // 2, D), BF16),
            pltpu.VMEM((R // 2, 2 * W), BF16),
            dma((M,)), dma((M,)),
            dma((M, NC)), dma((M, NC)),
            dma((6, M, M + 3)), dma((6, M, 2)),
            dma((E,)), dma((E,)),
            dma((M, NC)), dma((M, NC)),
            dma((E,)), dma((E,)),
            dma((E, M - 1)), dma((E, M)),
            dma((2, AC)), dma((AC,)),
            dma((6,)), dma((2,)), dma((6,)),
        ],
        compiler_params=pltpu.CompilerParams(collective_id=0, has_side_effects=True),
    )(
        x, mirror.reshape(1, R), slot, owner.reshape(1, G), window.reshape(1, G),
        up_e, down_e, mix_s, mix_m, up_a, down_a, gain.reshape(1, D),
    )


def solution(mesh):
    E, M = mesh.shape["edge"], mesh.shape["mp"]
    in_specs = (
        P("edge", "mp"),
        P("edge"),
        P("edge", None),
        P("edge", None),
        P("edge"),
        P(None, "mp"),
        P("mp", None),
        P(None, "mp"),
        P(None, "mp"),
        P(None, "mp"),
        P("mp", None),
        P(),
    )
    return jax.shard_map(
        functools.partial(body, E, M),
        mesh=mesh, in_specs=in_specs, out_specs=P("edge", "mp"), check_vma=False,
    )
```

```python
import functools
import jax
import jax.numpy as jnp
from jax import lax
from jax.experimental import pallas as pl
from jax.experimental.pallas import tpu as pltpu
from jax.sharding import PartitionSpec as P

AW = 16
MESH = pl.DeviceIdType.MESH
F32 = jnp.float32
BF16 = jnp.bfloat16


def iota(shape, dim):
    return lax.broadcasted_iota(jnp.int32, shape, dim)


def one_hot(mask):
    return jnp.where(mask, 1.0, 0.0).astype(BF16)


def dot(a, b):
    return jnp.dot(a, b, preferred_element_type=F32)


def silu(v):
    return v / (1.0 + jnp.exp(-v))


def at(start, size):
    return pl.ds(pl.multiple_of(start, size), size)


def kernel(
    E, M, cap,
    x_in, mirror_in, slot_in, owner_in, window_in,
    up_e, down_e, mix_s, mix_m, up_a, down_a, gain_in,
    out,
    x, mirror, slot, owner_r, window_r, gain,
    perm, own, rev, g_up_e, g_down_e, g_mix_s, g_mix_m, g_up_a, g_down_a,
    one, mixed_self, part, part_cols, idx_send, idx_got, select, block_send, block_got,
    total, atom_rows, updated,
    own_s, own_r, rev_s, rev_r, w_s, w_r, idx_s, idx_r, part_s, part_r,
    block_s, block_r, relay_s, relay_r, out_s, out_r, local_w, local, load,
):
    R, W = x.shape
    Q, D = R // M, W * M
    CH = slot.shape[1]
    NC = Q // CH
    G = owner_r.shape[1]
    GR = R // G
    PR = CH // GR * AW
    NP = NC * PR
    PF = M * NP
    SR = cap * AW
    half = Q // 2
    RH = R // 2
    AC = RH // half
    e, m = lax.axis_index("edge"), lax.axis_index("mp")
    p = e ^ (E // 2)
    side, pair = m % 2, m // 2
    peers = sorted(range(1, M), reverse=True)

    def remote(src, dst, ss, rs, f, j):
        return pltpu.make_async_remote_copy(
            src_ref=src, dst_ref=dst, send_sem=ss, recv_sem=rs,
            device_id=(f, j), device_id_type=MESH,
        )

    loads = [
        pltpu.make_async_copy(src, dst, load.at[i])
        for i, (src, dst) in enumerate(
            [
                (mirror_in, mirror), (x_in, x), (owner_in, owner_r),
                (window_in, window_r), (slot_in, slot), (gain_in, gain),
            ]
        )
    ]
    for copy in loads:
        copy.start()

    barrier = pltpu.get_barrier_semaphore()
    for d in peers:
        pl.semaphore_signal(barrier, inc=1, device_id=(p, m ^ d), device_id_type=MESH)
        pl.semaphore_signal(barrier, inc=1, device_id=(e, m ^ d), device_id_type=MESH)

    def greet(d, _):
        pl.semaphore_signal(barrier, inc=1, device_id=(e ^ d, m), device_id_type=MESH)
        return 0

    lax.fori_loop(1, E, greet, 0)

    shards = (up_e, down_e, mix_s, mix_m, up_a, down_a)
    wholes = (g_up_e, g_down_e, g_mix_s, g_mix_m, g_up_a, g_down_a)
    by_rows = (False, True, False, False, False, True)
    bits = [1 << b for b in reversed(range(M.bit_length() - 1))]

    def low_bits(d):
        return [b for b in bits if d == 0 or b < (d & -d)]

    high = [b for b in bits if b > 1]
    even = sorted(range(2, M, 2), key=lambda v: -(v & -v))
    mine, other = e % 2, 1 - e % 2
    swapped = (0, 1, 2, 3)

    def shard_at(k, i):
        if by_rows[k]:
            return wholes[k].at[at(i * W, W), :]
        return wholes[k].at[:, at(i * W, W)]

    def half_at(k, i, h):
        if by_rows[k]:
            return wholes[k].at[pl.ds(pl.multiple_of(i * W + h * (W // 2), W // 2), W // 2), :]
        return wholes[k].at[at(h * (D // 2), D // 2), at(i * W, W)]

    def w_near(k):
        return remote(shards[k], shard_at(k, m), w_s.at[k, 0, 1], w_r.at[k, 1, 0], e, m ^ 1)

    def w_far(k, d, b):
        if k not in swapped:
            src = shard_at(k, m ^ d) if d else shards[k]
            return remote(
                src, shard_at(k, m ^ d), w_s.at[k, d, b], w_r.at[k, d ^ b, 0], e, m ^ b
            )
        if d:
            src = half_at(k, m ^ d, mine)
        else:
            rows = shards[k].shape[0] // 2
            src = shards[k].at[at(mine * rows, rows), :]
        return remote(
            src, half_at(k, m ^ d, mine), w_s.at[k, d, b], w_r.at[k, d ^ b, 0], e, m ^ b
        )

    def w_swap(k, d):
        ref = half_at(k, m ^ d, mine)
        return remote(ref, ref, w_s.at[k, d, M], w_r.at[k, d, 1], e ^ 1, m)

    def w_pass(k, d, j):
        if k not in swapped:
            ref = shard_at(k, m ^ d)
        else:
            ref = half_at(k, m ^ d, other if j else mine)
        return remote(ref, ref, w_s.at[k, d, M + 1 + j], w_r.at[k, d ^ 1, j], e, m ^ 1)

    def w_own(k):
        return pltpu.make_async_copy(shards[k], shard_at(k, m), local_w.at[k])

    def w_start(k):
        for b in high:
            w_far(k, 0, b).start()
        w_near(k).start()

    def w_finish(k):
        for d in even:
            b = d & -d
            w_far(k, d ^ b, b).wait_recv()
            if k in swapped:
                w_swap(k, d).start()
            for c in high:
                if c < b:
                    w_far(k, d, c).start()
            w_pass(k, d, 0).start()

    def w_second(k):
        for d in even if k in swapped else ():
            w_swap(k, d).wait_recv()
            w_pass(k, d, 1).start()

    def w_wait(k):
        w_own(k).wait()
        w_near(k).wait_recv()
        for d in even:
            for j in range(1 + (k in swapped)):
                w_pass(k, d, j).wait_recv()

    def w_drain(k):
        w_near(k).wait_send()
        for b in high:
            w_far(k, 0, b).wait_send()
        for d in even:
            if k in swapped:
                w_swap(k, d).wait_send()
            for c in high:
                if c < (d & -d):
                    w_far(k, d, c).wait_send()
            for j in range(1 + (k in swapped)):
                w_pass(k, d, j).wait_send()

    for k in range(6):
        w_own(k).start()

    def own_local():
        return pltpu.make_async_copy(x_in.at[at(m * Q, Q), :], own.at[:, at(m * W, W)], local.at[0])

    def own_copy(d):
        return remote(
            x_in.at[at((m ^ d) * Q, Q), :], own.at[:, at(m * W, W)],
            own_s.at[d], own_r.at[d], e, m ^ d,
        )

    own_local().start()

    def rev_build(c):
        for j in range(M):
            rows = j * Q + c * CH
            picks = one_hot(iota((CH, R), 0) + rows == mirror[...])
            perm[at(rows, CH), :] = dot(picks, x[...]).astype(BF16)

    def rev_copy(c, d):
        j = m ^ d
        return remote(
            perm.at[at(j * Q + c * CH, CH), :], rev.at[at(c * CH, CH), at(m * W, W)],
            rev_s.at[d, c], rev_r.at[d, c], p, j,
        )

    def rev_start(c):
        for d in [0] + peers[::-1]:
            rev_copy(c, d).start()

    for copy in loads:
        copy.wait()

    diag = iota((G, G), 0) == iota((G, G), 1)
    owner_c = jnp.sum(jnp.where(diag, owner_r[...], 0), axis=1, keepdims=True)
    k_g = lax.div(iota((G, G * AW), 1), AW)
    row_g = iota((G, G * AW), 0)
    owner_k = jnp.sum(jnp.where(k_g == row_g, owner_c, 0), axis=0, keepdims=True)
    rank_k = jnp.sum(
        jnp.where((owner_c == owner_k) & (row_g < k_g), 1, 0), axis=0, keepdims=True
    )
    target = (owner_k * cap + rank_k) * AW + lax.rem(iota((1, G * AW), 1), AW)
    window_c = jnp.sum(jnp.where(diag, window_r[...], 0), axis=1, keepdims=True)
    rank_c = jnp.sum(
        jnp.where((owner_c == owner_r[...]) & (iota((G, G), 1) < iota((G, G), 0)), 1, 0),
        axis=1, keepdims=True,
    )
    place_c = owner_c * cap + rank_c

    def atom_index(f):
        lane = iota((G, SR), 1)
        hit = place_c == f * cap + lax.div(lane, AW)
        value = jnp.sum(
            jnp.where(hit, window_c * AW + lax.rem(lane, AW) + 1, 0), axis=0, keepdims=True
        )
        return jnp.broadcast_to(value - 1, (8, SR))

    def idx_build(d, _):
        idx_send[e ^ d] = atom_index(e ^ d)
        return 0

    lax.fori_loop(1, E, idx_build, 0)
    idx_got[e] = atom_index(e)
    rev_build(0)

    pl.semaphore_wait(barrier, E - 1 + 2 * (M - 1))

    def idx_copy(d):
        return remote(
            idx_send.at[e ^ d, pl.ds(0, 1), :], idx_got.at[e, pl.ds(0, 1), :], idx_s.at[d], idx_r.at[d], e ^ d, m
        )

    def idx_start(d, _):
        idx_copy(d).start()
        return 0

    lax.fori_loop(1, E, idx_start, 0)

    rev_start(0)
    for d in peers:
        own_copy(d).start()
    w_start(0)
    w_start(1)
    rev_build(1)
    rev_start(1)
    for c in range(2, NC):
        rev_build(c)

    def select_build(f, _):
        select[at(f * SR, SR), :] = one_hot(iota((SR, PF), 0) + f * SR == target)
        return 0

    lax.fori_loop(0, E, select_build, 0)
    w_finish(0)
    w_finish(1)
    for c in range(2, NC - 1):
        rev_start(c)
    w_start(2)
    w_start(3)
    own_local().wait()
    for d in peers:
        own_copy(d).wait_recv()
    w_second(0)
    w_second(1)
    w_wait(0)
    w_wait(1)

    def edge_rows(rows):
        hidden = silu(dot(rows, g_up_e[...])).astype(BF16)
        return (rows.astype(F32) + dot(hidden, g_down_e[...])).astype(BF16)

    def own_step(i, _):
        one[at(i * half, half), :] = edge_rows(own[at(i * half, half), :])
        return 0

    lax.fori_loop(0, 2, own_step, 0)
    rev_start(NC - 1)
    w_finish(2)
    w_finish(3)
    w_second(2)
    w_second(3)
    w_wait(2)

    def self_step(i, _):
        mixed_self[at(i * half, half), :] = dot(one[at(i * half, half), :], g_mix_s[...])
        return 0

    lax.fori_loop(0, 2, self_step, 0)
    w_wait(3)

    def part_copy(c, d):
        return remote(
            part.at[at(c * PR, PR), at((m ^ d) * W, W)],
            part_cols.at[at(m * NP + c * PR, PR), :],
            part_s.at[d, c], part_r.at[d, c], e, m ^ d,
        )

    def part_local(c):
        return pltpu.make_async_copy(
            part.at[at(c * PR, PR), at(m * W, W)],
            part_cols.at[at(m * NP + c * PR, PR), :], part_s.at[0, c],
        )

    def edge_step(c, _):
        for d in peers + [0]:
            rev_copy(c, d).wait_recv()
        rows = at(c * CH, CH)
        reverse = edge_rows(rev[rows, :])
        mixed = mixed_self[rows, :] + dot(reverse, g_mix_m[...])
        two = (one[rows, :].astype(F32) + silu(mixed)).astype(BF16)
        spot = lax.div(iota((PR, CH), 1), GR) * AW + slot[pl.ds(m * NC + c, 1), :]
        part[at(c * PR, PR), :] = dot(one_hot(iota((PR, CH), 0) == spot), two).astype(BF16)
        part_local(c).start()
        for d in peers:
            part_copy(c, d).start()
        return 0

    lax.fori_loop(0, NC - 1, edge_step, 0)
    edge_step(NC - 1, 0)
    w_start(4)
    w_start(5)

    def part_wait(c, _):
        part_local(c).wait()
        for d in peers:
            part_copy(c, d).wait_recv()
        return 0

    lax.fori_loop(0, NC, part_wait, 0)

    def owner_block(f):
        return dot(select[at(f * SR, SR), :], part_cols[...]).astype(BF16)

    def block_at(f, i):
        return block_got.at[at(f * SR, SR), at(i * W, W)]

    def block_copy(d):
        return remote(
            block_send.at[e ^ d], block_at(e, m), block_s.at[d], block_r.at[d], e ^ d, m
        )

    def block_step(d, _):
        block_send[e ^ d] = owner_block(e ^ d)
        block_copy(d).start()
        return 0

    lax.fori_loop(1, E, block_step, 0)
    block_got[at(e * SR, SR), at(m * W, W)] = owner_block(e)

    hops = [(j, b) for j in range(M) for b in low_bits(j)]

    def relay(d, j, b):
        ref = block_at(e ^ d, m ^ j)
        return remote(
            ref, ref, relay_s.at[d, hops.index((j, b))], relay_r.at[d, j ^ b], e, m ^ b
        )

    def relay_first(d):
        for b in low_bits(0):
            relay(d, 0, b).start()

    def relay_next(d):
        for j in sorted(range(1, M), key=lambda v: -(v & -v)):
            if low_bits(j):
                b = j & -j
                relay(d, j ^ b, b).wait_recv()
                for c in low_bits(j):
                    relay(d, j, c).start()

    def relay_wait(d):
        for j in range(1, M):
            if not low_bits(j):
                b = j & -j
                relay(d, j ^ b, b).wait_recv()

    def arrive(d):
        idx_copy(d).wait_recv()
        block_copy(d).wait_recv()
        relay_first(d)

    def placed(d, start):
        f = e ^ d
        picks = one_hot(iota((half, SR), 0) + start == idx_got[f][:1, :])
        return dot(picks, block_got[at(f * SR, SR), :])

    def gather(i):
        relay_wait(2 * i)
        relay_wait(2 * i + 1)

    def add(i):
        gather(i)

        def add_rows(r, _):
            start = side * RH + r * half
            rows = at(r * half, half)
            total[rows, :] += placed(2 * i, start) + placed(2 * i + 1, start)
            return 0

        lax.fori_loop(0, AC, add_rows, 0)

    def clear(r, _):
        total[at(r * half, half), :] = jnp.zeros((half, D), F32)
        return 0

    relay_first(0)
    lax.fori_loop(0, AC, clear, 0)
    arrive(1)
    last = E // 2 - 1

    def stage(i):
        arrive(2 * i + 2)
        arrive(2 * i + 3)
        relay_next(2 * i)
        relay_next(2 * i + 1)

    def flow(i, _):
        stage(i)
        add(i - 1)
        return 0

    stage(0)
    w_finish(4)
    w_finish(5)
    w_second(4)
    w_second(5)
    lax.fori_loop(1, last, flow, 0)
    add(last - 1)
    relay_next(2 * last)
    relay_next(2 * last + 1)
    w_wait(4)
    w_wait(5)
    gather(last)

    def out_rows(r, s):
        return out.at[at(s * RH + r * half, half), :]

    def out_copy(r):
        return remote(
            updated.at[at(r * half, half), at((1 - side) * W, W)], out_rows(r, side),
            out_s.at[1, r], out_r.at[r], e, m ^ 1,
        )

    def out_local(r):
        return pltpu.make_async_copy(
            updated.at[at(r * half, half), at(side * W, W)], out_rows(r, side), out_s.at[0, r]
        )

    def atom_step(r, _):
        rows = at(r * half, half)
        start = side * RH + r * half
        sums = total[rows, :] + (placed(2 * last, start) + placed(2 * last + 1, start))
        atom_rows[rows, :] = sums.astype(BF16)
        atoms = atom_rows[rows, :].astype(F32)
        scale = lax.rsqrt(jnp.sum(atoms * atoms, axis=1, keepdims=True) / D + 1e-06)
        normed = (atoms * scale * gain[...]).astype(BF16)
        hidden = silu(dot(normed, g_up_a[...])).astype(BF16)
        columns = at(pair * (2 * W), 2 * W)
        kept = atom_rows[rows, columns].astype(F32)
        updated[rows, :] = (kept + dot(hidden, g_down_a[:, columns])).astype(BF16)
        out_copy(r).start()
        out_local(r).start()
        return 0

    lax.fori_loop(0, AC, atom_step, 0)

    for d in peers:
        own_copy(d).wait_send()
    for k in range(6):
        w_drain(k)

    def drain_chunk(c, _):
        for d in peers + [0]:
            rev_copy(c, d).wait_send()
        for d in peers:
            part_copy(c, d).wait_send()
        return 0

    lax.fori_loop(0, NC, drain_chunk, 0)

    def drain_relay(d):
        for j, b in hops:
            relay(d, j, b).wait_send()

    def drain_owner(d, _):
        idx_copy(d).wait_send()
        block_copy(d).wait_send()
        drain_relay(d)
        return 0

    drain_relay(0)
    lax.fori_loop(1, E, drain_owner, 0)
    for r in range(AC):
        out_local(r).wait()
        out_copy(r).wait_send()
        out_copy(r).wait_recv()


def body(E, M, x, mirror, slot, owner, window, up_e, down_e, mix_s, mix_m, up_a, down_a, gain):
    R, W = x.shape
    Q, D = R // M, W * M
    NC = Q // slot.shape[1]
    G = owner.shape[0]
    anywhere = pl.BlockSpec(memory_space=pl.ANY)
    cap = max(2, 2 * G // E)
    SR = cap * AW
    NP = Q // (R // G) * AW
    AC = R // 2 // (Q // 2)
    vmem = pl.BlockSpec(memory_space=pl.ANY)
    dma = pltpu.SemaphoreType.DMA
    return pl.pallas_call(
        functools.partial(kernel, E, M, cap),
        name="edge_window",
        out_shape=jax.ShapeDtypeStruct((R, W), BF16),
        in_specs=[anywhere] * 12,
        out_specs=vmem,
        scratch_shapes=[
            pltpu.VMEM((R, W), BF16),
            pltpu.VMEM((1, R), jnp.int32),
            pltpu.VMEM(slot.shape, jnp.int32),
            pltpu.VMEM((1, G), jnp.int32),
            pltpu.VMEM((1, G), jnp.int32),
            pltpu.VMEM((1, D), F32),
            pltpu.VMEM((R, W), BF16),
            pltpu.VMEM((Q, D), BF16),
            pltpu.VMEM((Q, D), BF16),
        ]
        + [pltpu.VMEM((D, D), BF16)] * 6
        + [
            pltpu.VMEM((Q, D), BF16),
            pltpu.VMEM((Q, D), F32),
            pltpu.VMEM((NP, D), BF16),
            pltpu.VMEM((M * NP, W), BF16),
            pltpu.VMEM((E, 8, SR), jnp.int32),
            pltpu.VMEM((E, 8, SR), jnp.int32),
            pltpu.VMEM((E * SR, M * NP), BF16),
            pltpu.VMEM((E, SR, W), BF16),
            pltpu.VMEM((E * SR, D), BF16),
            pltpu.VMEM((R // 2, D), F32),
            pltpu.VMEM((R // 2, D), BF16),
            pltpu.VMEM((R // 2, 2 * W), BF16),
            dma((M,)), dma((M,)),
            dma((M, NC)), dma((M, NC)),
            dma((6, M, M + 3)), dma((6, M, 2)),
            dma((E,)), dma((E,)),
            dma((M, NC)), dma((M, NC)),
            dma((E,)), dma((E,)),
            dma((E, M - 1)), dma((E, M)),
            dma((2, AC)), dma((AC,)),
            dma((6,)), dma((2,)), dma((6,)),
        ],
        compiler_params=pltpu.CompilerParams(collective_id=0, has_side_effects=True),
    )(
        x, mirror.reshape(1, R), slot, owner.reshape(1, G), window.reshape(1, G),
        up_e, down_e, mix_s, mix_m, up_a, down_a, gain.reshape(1, D),
    )


def solution(mesh):
    E, M = mesh.shape["edge"], mesh.shape["mp"]
    in_specs = (
        P("edge", "mp"),
        P("edge"),
        P("edge", None),
        P("edge", None),
        P("edge"),
        P(None, "mp"),
        P("mp", None),
        P(None, "mp"),
        P(None, "mp"),
        P(None, "mp"),
        P("mp", None),
        P(),
    )
    return jax.shard_map(
        functools.partial(body, E, M),
        mesh=mesh, in_specs=in_specs, out_specs=P("edge", "mp"), check_vma=False,
    )
```
